32 devices in a mesh: blk: 8 (over z, x), head: 4 (over y, core).
Axes of the slice: x: 2, y: 2, z: 4, core: 2. Of those that a mesh axis runs over, the one named last changes fastest.
Arguments:
- layer_input: bfloat16 [4096, 5120], P(('blk', 'head')), may hold values from -0.1875 to 0.1875
- queries: bfloat16 [4096, 20, 128], P(('blk', 'head')), may hold values from -2 to 2
- key_vectors: bfloat16 [4096, 20, 128], P(('blk', 'head')), may hold values from -2 to 2
- value_vectors: bfloat16 [4096, 20, 128], P(('blk', 'head')), may hold values from -6 to 6
- out_grad: bfloat16 [4096, 20, 128], P(('blk', 'head')), may hold values from -24 to 24
- attn_out: bfloat16 [4096, 20, 128], P(('blk', 'head')), may hold values from -1.796875 to 1.796875
- log_sum: float32 [4096, 20], P(('blk', 'head')), may hold values from 5.5 to 8
- block_list: int32 [32, 8], replicated, may hold values from -1 to 31, as said below
Outputs:
- query_grad: bfloat16 [4096, 20, 128], P(('blk', 'head'))
- key_grad: bfloat16 [4096, 20, 128], P(('blk', 'head'))
- weight_grad: float32 [5120, 2560], P('blk', 'head')
The draws below stay inside these ranges and needn't reach their ends.
Inputs may be any that keep to these rules, and one draw needn't show every extreme that they name: `block_list`: row r lists distinct key blocks c (blocks of 128 tokens) with |c // 4 - r // 4| <= 1, block r among them, followed by -1 in the unused slots; some row uses all 8 slots.
All inputs are finite; a program needn't handle non-finite values.
Results may differ from the reference program's by a relative error of at most 0.0051.
Values may be sent and summed in bfloat16 or wider, within the bound.
No kernel may reach another device: no remote copies, remote signals or barrier semaphores. Data moves between devices by JAX's collectives and lax.ppermute only.
A program may use at most 128 MiB of HBM per device.

```python
import jax
import jax.numpy as jnp
from jax import lax

D = 5120
H = 20
HD = 128
BLOCK = 128
KB = 8
BLOCKS_DEV = 4
TOKENS = 4096
N_BLK = 8


def draw_block_list(key, part):
    groups = N_BLK
    blocks = TOKENS // BLOCK
    split_keys = jax.random.split(jax.random.fold_in(key, 11), 5)
    device_ids = jnp.arange(groups)
    special = jax.random.randint(split_keys[2], (), 1, groups - 1)
    forced = (jnp.minimum(device_ids, groups - 1 - device_ids) <= 1) | (jnp.abs(device_ids - groups // 2) <= 1) | (device_ids == special)
    left_open = (jax.random.randint(split_keys[0], (groups,), 0, 4) > 0) | forced
    right_open = (jax.random.randint(split_keys[1], (groups,), 0, 4) > 0) | forced
    block_ids = jnp.arange(blocks)
    owner = block_ids // BLOCKS_DEV
    offset = owner[None, :] - owner[:, None]
    allowed = (offset == 0) | (offset == -1) & left_open[owner][:, None] | (offset == 1) & right_open[owner][:, None]
    distance = jnp.abs(block_ids[None, :] - block_ids[:, None])
    noise = jax.random.randint(split_keys[3], (blocks, blocks), 0, 4096)
    priority = noise - 1024 * distance + jnp.where(distance == 0, 1 << 20, 0) + jnp.where(distance == 1, 1 << 19, 0)
    priority = jnp.where(allowed, priority, -(1 << 30))
    ranked = jnp.argsort(-priority, axis=1, stable=True)[:, :KB]
    wanted = jax.random.randint(split_keys[4], (blocks,), 3, KB + 1)
    wanted = jnp.where(block_ids == special * BLOCKS_DEV, KB, wanted)
    wanted = jnp.minimum(wanted, jnp.sum(allowed.astype(jnp.int32), axis=1))
    slot_ids = jnp.arange(KB)
    return jnp.where(slot_ids[None, :] < wanted[:, None], ranked, -1).astype(jnp.int32)


def spiked(result, stream_key, source, target, shards_of, factor):
    owner, partner = [(jnp.arange(result.shape[dim]) // (result.shape[dim] // shards_of)).reshape([-1 if axis == dim else 1 for axis in range(result.ndim)]) for dim in (source, target)]
    chosen = jax.random.permutation(stream_key, shards_of)[partner]
    strong = (owner == chosen) | (owner == (partner + shards_of // 2) % shards_of)
    return jnp.where(strong, factor * result, result)


def steps_of(key, dims, cuts, least, largest):
    def one(dim, parts):
        draws = jax.random.uniform(jax.random.fold_in(jax.random.fold_in(key, 6), dim), (parts,), jnp.float32, least / len(cuts), largest / len(cuts))
        return jnp.repeat(jnp.exp(draws), dims[dim] // parts).reshape((-1,) + (1,) * (len(dims) - dim - 1))

    factor_of = one(*cuts[0])
    for cut in cuts[1:]:
        factor_of = factor_of * one(*cut)
    return factor_of


def centred(stream_key, extent, scale, most, cuts=(), kind=jnp.bfloat16):
    loudness = steps_of(stream_key, extent, cuts, -0.22, 0.18) if cuts else 1.0
    result = jax.random.normal(stream_key, extent, jnp.float32) * scale * loudness
    return jnp.minimum(jnp.maximum(result, -most), most).astype(kind)


def heavy_noise(own_key, dims, deviation, bound, pieces, heavy, kind=jnp.bfloat16):
    drawn = deviation * jax.random.normal(own_key, dims, jnp.float32)
    if pieces:
        drawn = drawn * steps_of(own_key, dims, pieces, -0.22, 0.18)
    return jnp.clip(spiked(drawn, jax.random.fold_in(own_key, 3), *heavy), -bound, bound).astype(kind)


def setup_inputs(seed: int = 0) -> dict:
    arg_keys = jax.random.split(jax.random.key(seed), 9)
    layer_input = heavy_noise(arg_keys[0], (TOKENS, D), TOKENS ** -0.5, 0.1875, ((0, 32),), (0, 1, 32, 2.75))
    queries = jnp.clip(jax.random.uniform(arg_keys[1], (TOKENS, H, HD), jnp.float32, -2.0, 2.0) * steps_of(arg_keys[1], (TOKENS, H, HD), ((0, 32),), -0.4, 0.0), -2.0, 2.0).astype(jnp.bfloat16)
    key_vectors = jnp.clip(jax.random.uniform(arg_keys[2], (TOKENS, H, HD), jnp.float32, -2.0, 2.0) * steps_of(arg_keys[2], (TOKENS, H, HD), ((0, 32),), -0.4, 0.0), -2.0, 2.0).astype(jnp.bfloat16)
    value_vectors = centred(arg_keys[3], (TOKENS, H, HD), 1.0, 6.0, ((0, 32),))
    out_grad = centred(arg_keys[4], (TOKENS, H, HD), 4.0, 24.0, ((0, 32),))
    attn_out = centred(arg_keys[5], (TOKENS, H, HD), 0.3, 1.796875, ((0, 32),))
    log_sum = jnp.clip(5.5 + 2.5 * jax.random.uniform(arg_keys[6], (TOKENS, H), jnp.float32) ** steps_of(arg_keys[6], (TOKENS, H), ((0, 32),), -0.2, 0.2), 5.5, 8.0)
    block_list = draw_block_list(jax.random.fold_in(arg_keys[8], 71), 0)
    return dict(layer_input=layer_input, queries=queries, key_vectors=key_vectors, value_vectors=value_vectors, out_grad=out_grad, attn_out=attn_out, log_sum=log_sum, block_list=block_list)


def reference(layer_input, queries, key_vectors, value_vectors, out_grad, attn_out, log_sum, block_list):
    score_scale = HD ** -0.5
    row_delta = jnp.sum(out_grad.astype(jnp.float32) * attn_out.astype(jnp.float32), axis=2)
    block_total = TOKENS // BLOCK
    key_blocks = key_vectors.reshape(block_total, BLOCK, H, HD)
    value_blocks = value_vectors.reshape(block_total, BLOCK, H, HD)

    def one_block(carry, block_index):
        key_acc, value_acc = carry
        listed = block_list[block_index]
        present = (listed >= 0).astype(jnp.float32)
        chosen = jnp.where(listed >= 0, listed, 0).astype(jnp.int32)
        first_row = (block_index * BLOCK).astype(jnp.int32)
        query_rows = lax.dynamic_slice_in_dim(queries, first_row, BLOCK, 0).astype(jnp.float32)
        grad_rows = lax.dynamic_slice_in_dim(out_grad, first_row, BLOCK, 0).astype(jnp.float32)
        lse_rows = lax.dynamic_slice_in_dim(log_sum, first_row, BLOCK, 0)
        delta_rows = lax.dynamic_slice_in_dim(row_delta, first_row, BLOCK, 0)
        key_chosen = key_blocks[chosen].astype(jnp.float32)
        value_chosen = value_blocks[chosen].astype(jnp.float32)
        scores = jnp.einsum("qhd,jkhd->hqjk", query_rows, key_chosen) * score_scale
        weights = jnp.exp(scores - lse_rows.T[:, :, None, None]) * present[None, None, :, None]
        weights_b = lax.optimization_barrier(weights.astype(jnp.bfloat16)).astype(jnp.float32)
        dweights = jnp.einsum("qhd,jkhd->hqjk", grad_rows, value_chosen)
        dscores = weights * (dweights - delta_rows.T[:, :, None, None])
        dscores_b = lax.optimization_barrier(dscores.astype(jnp.bfloat16)).astype(jnp.float32)
        query_part = jnp.einsum("hqjk,jkhd->qhd", dscores_b, key_chosen) * score_scale
        key_part = jnp.einsum("hqjk,qhd->jkhd", dscores_b, query_rows) * score_scale
        value_part = jnp.einsum("hqjk,qhd->jkhd", weights_b, grad_rows)
        key_acc = key_acc.at[chosen].add(key_part)
        value_acc = value_acc.at[chosen].add(value_part)
        return (key_acc, value_acc), query_part

    zeros_acc = jnp.zeros((block_total, BLOCK, H, HD), jnp.float32)
    (key_acc, value_acc), query_parts = lax.scan(one_block, (zeros_acc, zeros_acc), jnp.arange(block_total, dtype=jnp.int32))
    query_grad = query_parts.reshape(TOKENS, H, HD).astype(jnp.bfloat16)
    key_grad = key_acc.reshape(TOKENS, H, HD).astype(jnp.bfloat16)
    value_grad = value_acc.reshape(TOKENS, H * HD).astype(jnp.bfloat16)
    weight_grad = jnp.dot(layer_input.T, value_grad, preferred_element_type=jnp.float32)
    return (query_grad, key_grad, weight_grad)
```

```python
import functools
import math

import jax
import jax.numpy as jnp
from jax import lax
from jax.experimental import pallas as pl
from jax.experimental.pallas import tpu as pltpu
from jax.sharding import PartitionSpec as P

AXES = ("blk", "head")
STAT_ROWS = 32
MASKED = 1e30
F32 = jnp.float32
BF16 = jnp.bfloat16
VM = pl.BlockSpec(memory_space=pltpu.VMEM)
SM = pl.BlockSpec(memory_space=pltpu.SMEM)


def call(kernel, name, args, outs, scratch=(), flops=0, smem=1):
    moved = sum(a.size * a.dtype.itemsize for a in args) + sum(
        math.prod(o.shape) * o.dtype.itemsize for o in outs
    )
    return pl.pallas_call(
        kernel,
        name=name,
        out_shape=tuple(outs),
        in_specs=[SM] * smem + [VM] * (len(args) - smem),
        out_specs=tuple(VM for _ in outs),
        scratch_shapes=list(scratch),
        cost_estimate=pl.CostEstimate(flops=flops, bytes_accessed=moved, transcendentals=0),
    )(*args)


class Plan:
    def __init__(self, n_blk, n_head, group, block, dim):
        self.n_blk, self.n_head = n_blk, n_head
        self.planes = n_blk // 2
        self.group, self.half, self.slots = group, group // 2, group // 2 + 1
        self.block, self.dim = block, dim
        self.span = block * n_head
        self.units = [(s, 0) for s in range(self.slots)] + [(s, 1) for s in range(self.half)]

    def perm(self, move):
        pairs = []
        for z in range(self.planes):
            for x in range(2):
                for h in range(self.n_head):
                    target = move(z, x, h)
                    if target is not None and 0 <= target[0] < self.planes:
                        tz, tx, th = target
                        pairs.append(
                            ((2 * z + x) * self.n_head + h, (2 * tz + tx) * self.n_head + th)
                        )
        return pairs

    def send(self, value, move):
        return lax.ppermute(value, AXES, self.perm(move))

    def partner(self, value, i, k):
        return self.send(value, lambda z, x, h: (z, x ^ i, h ^ k))

    def head_of(self, x, slot):
        if slot == self.half:
            return self.half
        return (self.half + 1) * x + slot


def pack_queries(plan, scal, q, g, a, lse):
    group, half, slots, block, dim = plan.group, plan.half, plan.slots, plan.block, plan.dim
    heads = q.shape[0]
    log2e = 1.0 / math.log(2.0)

    def kernel(scal_ref, q_ref, g_ref, a_ref, lse_ref, *rest):
        outs, parts = rest[:-1], rest[-1]
        x, h = scal_ref[1], scal_ref[2]
        delta = jnp.sum(g_ref[...].astype(F32) * a_ref[...].astype(F32), axis=2)
        for t, stat in enumerate((lse_ref[...] * log2e, delta)):
            high = stat.astype(BF16).astype(F32)
            rest_ = stat - high
            mid = rest_.astype(BF16).astype(F32)
            parts[t * 3, :, :] = high
            parts[t * 3 + 1, :, :] = mid
            parts[t * 3 + 2, :, :] = rest_ - mid
        pad = jnp.zeros((STAT_ROWS - 6 * slots, block), F32)
        for i in range(2):
            for k in range(plan.n_head):
                out = outs[i * plan.n_head + k]
                base = (h ^ k) * group
                rows = []
                for s in range(slots):
                    head = base + plan.head_of(x ^ i, s)
                    start = STAT_ROWS + s * 2 * block
                    out[start : start + block, :] = q_ref[head]
                    out[start + block : start + 2 * block, :] = g_ref[head]
                    rows += [parts[t, pl.ds(head, 1), :] for t in range(6)]
                out[0:STAT_ROWS, :] = jnp.concatenate(rows + [pad], axis=0).astype(BF16)

    shape = jax.ShapeDtypeStruct((STAT_ROWS + slots * 2 * block, dim), BF16)
    return call(
        kernel,
        "pack_queries",
        (scal, q, g, a, lse),
        [shape] * (2 * plan.n_head),
        [pltpu.VMEM((6, heads, block), F32)],
    )


def pack_keys(plan, scal, key, val):
    group, half, slots, block, dim = plan.group, plan.half, plan.slots, plan.block, plan.dim

    def kernel(scal_ref, k_ref, v_ref, *outs):
        x, h = scal_ref[1], scal_ref[2]
        for i in range(2):
            for k in range(plan.n_head):
                out = outs[i * plan.n_head + k]
                for s in range(slots if i == 0 else half):
                    head = (h ^ k) * group + plan.head_of(x ^ i, s)
                    out[s * 2 * block : (s * 2 + 1) * block, :] = k_ref[head]
                    out[(s * 2 + 1) * block : (s * 2 + 2) * block, :] = v_ref[head]

    own = jax.ShapeDtypeStruct((slots * 2 * block, dim), BF16)
    other = jax.ShapeDtypeStruct((half * 2 * block, dim), BF16)
    return call(
        kernel, "pack_keys", (scal, key, val), [own] * plan.n_head + [other] * plan.n_head
    )


def gather_queries(plan, c, refs, q_s, g_s, lse_s, delta_s):
    n, block = plan.n_head, plan.block
    for r in range(4):
        for k in range(n):
            ref = refs[r * n + k]
            rows = pl.ds(pl.multiple_of((k ^ c) * block, block), block)
            stats = ref[0:STAT_ROWS, :].astype(F32)
            for s in range(plan.half if r == 3 else plan.slots):
                start = STAT_ROWS + s * 2 * block
                q_s[s * 4 + r, rows, :] = ref[start : start + block, :]
                g_s[s * 4 + r, rows, :] = ref[start + block : start + 2 * block, :]
                at = [stats[s * 6 + t : s * 6 + t + 1, :] for t in range(6)]
                lse_s[s * 4 + r, :, rows] = at[0] + (at[1] + at[2])
                delta_s[s * 4 + r, :, rows] = at[3] + (at[4] + at[5])


def gather_keys(plan, c, refs, which, out):
    n, block = plan.n_head, plan.block
    for u, (s, r) in enumerate(plan.units):
        for k in range(n):
            rows = pl.ds(pl.multiple_of((k ^ c) * block, block), block)
            start = (s * 2 + which) * block
            out[u, rows, :] = refs[r * n + k][start : start + block, :]


NT = (((1,), (1,)), ((), ()))


def unit_of(plan, u):
    late = (u >= plan.slots).astype(jnp.int32)
    return u - plan.slots * late, late


def weights_of(plan, mask_ref, scores, lse_row, rq, rk, half_span, scale):
    n, block = plan.n_head, plan.block
    per = n // 2
    pieces = []
    for pk in range(n):
        bias = jnp.concatenate(
            [
                jnp.full(
                    (1, block),
                    mask_ref[((rq * n + half_span * per + p) * 2 + rk) * n + pk],
                    F32,
                )
                for p in range(per)
            ],
            axis=1,
        )
        pieces.append(
            jnp.exp2(scores[pk * block : (pk + 1) * block, :] * scale - (lse_row + bias))
        )
    return jnp.concatenate(pieces, axis=0)


def value_terms(plan, scal, mask, windows, keys):
    n, block, dim, span = plan.n_head, plan.block, plan.dim, plan.span
    nu = len(plan.units)
    scale = dim**-0.5 / math.log(2.0)
    half_rows = span // 2

    def kernel(scal_ref, mask_ref, *rest):
        c = scal_ref[3]
        q_refs, k_refs = rest[: 4 * n], rest[4 * n : 6 * n]
        out, q_s, g_s, lse_s, delta_s, k_s = rest[6 * n :]
        gather_queries(plan, c, q_refs, q_s, g_s, lse_s, delta_s)
        gather_keys(plan, c, k_refs, 0, k_s)

        def body(u, carry):
            slot, rk = unit_of(plan, u)
            kb = k_s[u]
            total = jnp.zeros((span, dim), F32)
            for j in range(6):
                rq = rk + j // 2
                rows = slice((j % 2) * half_rows, (j % 2 + 1) * half_rows)
                qb = q_s[slot * 4 + rq, rows, :]
                gb = g_s[slot * 4 + rq, rows, :]
                scores = lax.dot_general(kb, qb, NT, preferred_element_type=F32)
                w = weights_of(
                    plan, mask_ref, scores, lse_s[slot * 4 + rq, :, rows], rq, rk, j % 2, scale
                )
                total += jnp.dot(w.astype(BF16), gb, preferred_element_type=F32)
            out[u] = total.T.astype(BF16)
            return carry

        lax.fori_loop(0, nu, body, 0)

    return call(
        kernel,
        "value_terms",
        (scal, mask, *windows, *keys),
        [jax.ShapeDtypeStruct((nu, dim, span), BF16)],
        [
            pltpu.VMEM((plan.slots * 4, span, dim), BF16),
            pltpu.VMEM((plan.slots * 4, span, dim), BF16),
            pltpu.VMEM((plan.slots * 4, 1, span), F32),
            pltpu.VMEM((plan.slots * 4, 1, span), F32),
            pltpu.VMEM((nu, span, dim), BF16),
        ],
        flops=nu * 2 * 2 * 3 * span * span * dim,
        smem=2,
    )[0]


def score_terms(plan, scal, mask, windows, keys):
    n, block, dim, span = plan.n_head, plan.block, plan.dim, plan.span
    nu = len(plan.units)
    score_scale = dim**-0.5
    scale = score_scale / math.log(2.0)
    half_rows = span // 2

    def kernel(scal_ref, mask_ref, *rest):
        c = scal_ref[3]
        q_refs, k_refs = rest[: 4 * n], rest[4 * n : 6 * n]
        near, far, mine, dk_out, q_s, g_s, lse_s, delta_s, k_s, v_s, dq_s = rest[6 * n :]
        gather_queries(plan, c, q_refs, q_s, g_s, lse_s, delta_s)
        gather_keys(plan, c, k_refs, 0, k_s)
        gather_keys(plan, c, k_refs, 1, v_s)
        dq_s[...] = jnp.zeros_like(dq_s)

        def body(u, carry):
            slot, rk = unit_of(plan, u)
            kb = k_s[u]
            vb = v_s[u]
            kt = kb.T
            total = jnp.zeros((span, dim), F32)
            for j in range(6):
                rq = rk + j // 2
                at = slot * 4 + rq
                rows = slice((j % 2) * half_rows, (j % 2 + 1) * half_rows)
                qb = q_s[at, rows, :]
                gb = g_s[at, rows, :]
                scores = lax.dot_general(kb, qb, NT, preferred_element_type=F32)
                w = weights_of(plan, mask_ref, scores, lse_s[at, :, rows], rq, rk, j % 2, scale)
                dw = lax.dot_general(vb, gb, NT, preferred_element_type=F32)
                ds = (w * (dw - delta_s[at, :, rows])).astype(BF16)
                total += jnp.dot(ds, qb, preferred_element_type=F32)
                dq_s[at, :, rows] += jnp.dot(kt, ds, preferred_element_type=F32)
            dk_out[u] = (total * score_scale).astype(BF16)
            return carry

        lax.fori_loop(0, nu, body, 0)
        for s in range(plan.slots):
            near[s] = (dq_s[s * 4].T * score_scale).astype(BF16)
            mine[s] = dq_s[s * 4 + 1].T * score_scale
            mine[plan.slots + s] = dq_s[s * 4 + 2].T * score_scale
            if s < plan.half:
                far[s] = (dq_s[s * 4 + 3].T * score_scale).astype(BF16)

    return call(
        kernel,
        "score_terms",
        (scal, mask, *windows, *keys),
        [
            jax.ShapeDtypeStruct((plan.slots, span, dim), BF16),
            jax.ShapeDtypeStruct((plan.half, span, dim), BF16),
            jax.ShapeDtypeStruct((2 * plan.slots, span, dim), F32),
            jax.ShapeDtypeStruct((nu, span, dim), BF16),
        ],
        [
            pltpu.VMEM((plan.slots * 4, span, dim), BF16),
            pltpu.VMEM((plan.slots * 4, span, dim), BF16),
            pltpu.VMEM((plan.slots * 4, 1, span), F32),
            pltpu.VMEM((plan.slots * 4, 1, span), F32),
            pltpu.VMEM((nu, span, dim), BF16),
            pltpu.VMEM((nu, span, dim), BF16),
            pltpu.VMEM((plan.slots * 4, dim, span), F32),
        ],
        flops=nu * 4 * 2 * 3 * span * span * dim,
        smem=2,
    )


def pack_returns(plan, scal, mine, near, far, dk):
    block, dim, slots, half = plan.block, plan.dim, plan.slots, plan.half

    def kernel(scal_ref, mine_ref, near_ref, far_ref, dk_ref, *outs):
        c = scal_ref[3]
        for i in range(2):
            for k in range(plan.n_head):
                out = outs[i * plan.n_head + k]
                rows = pl.ds(pl.multiple_of((k ^ c) * block, block), block)
                for s in range(slots):
                    total = mine_ref[i * slots + s, rows, :]
                    if i == 1:
                        total += near_ref[s, rows, :].astype(F32)
                    elif s < half:
                        total += far_ref[s, rows, :].astype(F32)
                    out[s] = total.astype(BF16)
                for s in range(slots if i == 0 else half):
                    out[slots + s] = dk_ref[i * slots + s, rows, :]

    own = jax.ShapeDtypeStruct((2 * slots, block, dim), BF16)
    other = jax.ShapeDtypeStruct((slots + half, block, dim), BF16)
    return call(
        kernel,
        "pack_returns",
        (scal, mine, near, far, dk),
        [own] * plan.n_head + [other] * plan.n_head,
    )


def unpack_returns(plan, scal, bufs):
    block, dim, slots, half, n = plan.block, plan.dim, plan.slots, plan.half, plan.n_head
    heads = n * plan.group

    def kernel(scal_ref, *rest):
        refs, (dq, dk) = rest[: 2 * n], rest[2 * n :]
        x, h = scal_ref[1], scal_ref[2]
        for k in range(n):
            base = (h ^ k) * plan.group
            for i in range(2):
                ref = refs[i * n + k]
                for s in range(half):
                    head = base + plan.head_of(x ^ i, s)
                    dq[head] = ref[s]
                    dk[head] = ref[slots + s]
            both = refs[k][half].astype(F32) + refs[n + k][half].astype(F32)
            dq[base + half] = both.astype(BF16)
            dk[base + half] = refs[k][slots + half]

    shape = jax.ShapeDtypeStruct((heads, block, dim), BF16)
    return call(kernel, "unpack_returns", (scal, *bufs), [shape, shape])


def split_rows(plan, scal, rows):
    tokens, width = rows.shape
    cols = width // plan.n_blk

    def kernel(scal_ref, in_ref, out_ref):
        out_ref[0, 0] = in_ref[...]

    return pl.pallas_call(
        kernel,
        name="split_rows",
        out_shape=jax.ShapeDtypeStruct((2, plan.planes, tokens, cols), BF16),
        grid_spec=pltpu.PrefetchScalarGridSpec(
            num_scalar_prefetch=1,
            grid=(2, plan.planes),
            in_specs=[
                pl.BlockSpec((tokens, cols), lambda l, k, sc: (0, 2 * (sc[0] ^ k) + (sc[3] ^ l)))
            ],
            out_specs=pl.BlockSpec((1, 1, tokens, cols), lambda l, k, sc: (l, k, 0, 0)),
        ),
        cost_estimate=pl.CostEstimate(
            flops=0, bytes_accessed=4 * rows.size, transcendentals=0
        ),
    )(scal, rows)


def spread_rows(plan, scal, rows):
    both = split_rows(plan, scal, rows)
    crossed = plan.partner(both[1], 0, 1)
    pieces = []
    for k in range(plan.planes):
        piece = jnp.stack((both[0, k], crossed[k]))
        if k:
            piece = plan.send(piece, lambda z, x, h, k=k: (z ^ k, x, h))
        pieces.append(piece)
    out = []
    for k, own in enumerate(pieces):
        by_x = plan.partner(own, 1, 0)
        by_y = plan.partner(own, 0, 2)
        both_ways = plan.partner(by_x, 0, 2) if k % 2 == 0 else plan.partner(by_y, 1, 0)
        out.append(((own, by_y), (by_x, both_ways)))
    return out


def order_rows(plan, scal, pieces):
    cols = pieces[0][0][0].shape[2]
    block = plan.block
    flat = [pieces[k][i][j] for k in range(plan.planes) for i in range(2) for j in range(2)]

    def kernel(scal_ref, *rest):
        refs, out = rest[:-1], rest[-1]
        c = scal_ref[3]
        for k in range(plan.planes):
            for i in range(2):
                for j in range(2):
                    ref = refs[(k * 2 + i) * 2 + j]
                    for l in range(2):
                        rows = pl.ds(pl.multiple_of((2 * j + (l ^ c)) * block, block), block)
                        out[k, i, rows, :] = ref[l]

    return call(
        kernel,
        "order_rows",
        (scal, *flat),
        [jax.ShapeDtypeStruct((plan.planes, 2, plan.span, cols), BF16)],
    )[0]


def weight_step(plan, info, total, rows, terms, name):
    cols = rows.shape[3]
    span, dim, slots = plan.span, plan.dim, plan.slots
    nu = len(plan.units)
    count = len(terms) // 2
    first = total is None
    out = jax.ShapeDtypeStruct((2, slots * dim, cols), F32)

    def kernel(info_ref, rows_ref, *rest):
        refs = rest[: 2 * count]
        out_ref = rest[-1]
        p, r = pl.program_id(0), pl.program_id(1)

        @pl.when((p == 0) & (r == 0))
        def _():
            out_ref[...] = jnp.zeros_like(out_ref) if first else rest[2 * count][...]

        x = rows_ref[0, 0]
        for index in range(count):
            for side in range(2):
                lo, hi = (0, slots) if side == 0 else (slots, nu)

                @pl.when((p == index) & (r == side) & (info_ref[2 + 2 * index] > 0))
                def _(index=index, lo=lo, hi=hi):
                    for l in range(2):
                        left = refs[2 * index + l][lo:hi].reshape((hi - lo) * dim, span)
                        part = jnp.dot(left, x, preferred_element_type=F32)
                        at = info_ref[0] ^ l
                        out_ref[at, 0 : (hi - lo) * dim, :] += part

    whole = pl.BlockSpec((nu, dim, span), lambda p, r, sc: (0, 0, 0))
    acc = pl.BlockSpec((2, slots * dim, cols), lambda p, r, sc: (0, 0, 0))
    args = list(terms) + ([] if first else [total])
    return pl.pallas_call(
        kernel,
        name=name,
        out_shape=out,
        grid_spec=pltpu.PrefetchScalarGridSpec(
            num_scalar_prefetch=1,
            grid=(count, 2),
            in_specs=[pl.BlockSpec((1, 1, span, cols), lambda p, r, sc: (sc[1 + 2 * p], r, 0, 0))]
            + [whole] * (2 * count)
            + ([] if first else [acc]),
            out_specs=acc,
        ),
        cost_estimate=pl.CostEstimate(
            flops=2 * nu * dim * span * cols * count,
            bytes_accessed=count * span * cols * 4 + 8 * slots * dim * cols * 2,
            transcendentals=0,
        ),
    )(info, rows, *args)


def finish_weights(plan, scal, near, far):
    wide, cols = near.shape
    pair, dim = plan.half * plan.dim, plan.dim

    def kernel(scal_ref, near_ref, far_ref, out):
        c = scal_ref[3]

        def write(low, high):
            out[:, 0:pair] = low[0:pair, :].astype(F32).T
            out[:, pair + dim :] = high[0:pair, :].astype(F32).T
            middle = low[pair:, :].astype(F32) + high[pair:, :].astype(F32)
            out[:, pair : pair + dim] = middle.T

        @pl.when(c == 0)
        def _():
            write(near_ref, far_ref)

        @pl.when(c == 1)
        def _():
            write(far_ref, near_ref)

    return call(
        kernel,
        "finish_weights",
        (scal, near, far),
        [jax.ShapeDtypeStruct((cols, 2 * pair + dim), F32)],
    )[0]


def weight_gradient(plan, scal, rows, own):
    z, x, c = scal[0], scal[1], scal[3]
    pieces = order_rows(plan, scal, spread_rows(plan, scal, rows))
    across = lambda v: plan.partner(v, 0, 1)
    one = jnp.ones((), jnp.int32)
    total = weight_step(
        plan, jnp.stack([x ^ c, 0 * z, one]), None, pieces, [own, across(own)], "weight_own"
    )
    up = down = own
    for step in range(1, plan.planes):
        up = plan.send(up, lambda z, x, h: (z + 1, x, h))
        down = plan.send(down, lambda z, x, h: (z - 1, x, h))
        below, above = z - step, z + step
        has_below = below >= 0
        has_above = above < plan.planes
        info = jnp.stack(
            [
                x ^ c,
                jnp.where(has_below, z ^ below, 0),
                has_below.astype(jnp.int32),
                jnp.where(has_above, z ^ above, 0),
                has_above.astype(jnp.int32),
            ]
        )
        total = weight_step(
            plan, info, total, pieces, [up, across(up), down, across(down)], f"weight_{step}"
        )
    half = total.astype(BF16)
    near = plan.send(half[0], lambda z, x, h: (z, h & 1, (h & ~1) | x))
    far = plan.send(half[1], lambda z, x, h: (z, h & 1, (h & ~1) | (x ^ 1)))
    return finish_weights(plan, scal, near, far)


def weight_gradient_summed(plan, scal, rows, own):
    h, x = scal[2], scal[1]
    half, slots, dim, span = plan.half, plan.slots, plan.dim, plan.span
    other = plan.partner(own[slots:], 1, 0)
    low = jnp.where(x == 0, own[:half], other)
    high = jnp.where(x == 0, other, own[:half])
    value = jnp.concatenate([low, own[half:slots], high], axis=0)
    value = value.reshape(plan.group * dim, plan.n_head, plan.block)
    places = jnp.arange(plan.n_head, dtype=jnp.int32) ^ (h & ~1)
    value = jnp.take(value, places, axis=1).reshape(plan.group * dim, span)
    gathered = lax.all_gather(rows, "head", axis=0, tiled=True)
    product = jnp.einsum("ts,ct->sc", gathered, value, preferred_element_type=F32)
    return lax.psum_scatter(product, "blk", scatter_dimension=0, tiled=True)


def local(n_blk, n_head, layer_input, queries, keys, values, out_grad, attn_out, log_sum, blocks):
    tokens, heads, dim = queries.shape
    plan = Plan(n_blk, n_head, heads // n_head, tokens, dim)
    n = n_head
    b, h = lax.axis_index("blk"), lax.axis_index("head")
    z, x, c = b // 2, b % 2, h % 2
    scal = jnp.stack([z, x, h, c]).astype(jnp.int32)
    z, x, h, c = scal[0], scal[1], scal[2], scal[3]
    by_head = lambda v: jnp.moveaxis(v, 1, 0)
    q, g, a, k, v = (by_head(m) for m in (queries, out_grad, attn_out, keys, values))

    places = jnp.arange(n, dtype=jnp.int32) ^ (h & ~1)
    spans = b + (1 - 2 * x) * jnp.arange(-1, 3, dtype=jnp.int32)
    query_ids = (spans[:, None] * n + places[None, :]).reshape(-1)
    key_ids = (spans[1:3, None] * n + places[None, :]).reshape(-1)
    inside = (query_ids >= 0) & (query_ids < blocks.shape[0])
    listed = blocks[jnp.where(inside, query_ids, 0)]
    linked = jnp.any(listed[:, None, :] == key_ids[None, :, None], axis=2) & inside[:, None]
    mask = jnp.where(linked, 0.0, MASKED).astype(F32).reshape(-1)

    sent = pack_queries(plan, scal, q, g, a, log_sum.T)
    windows = {(0, 0): sent[0]}
    order = [(1, kk) for kk in range(n)] + [(0, kk) for kk in range(1, n)]
    for i, kk in order:
        windows[i, kk] = plan.partner(sent[i * n + kk], i, kk)
    pair_rows = STAT_ROWS + plan.half * 2 * tokens
    near = [
        plan.send(windows[1, kk], lambda z, x, h: (z + 1 - 2 * x, x, h)) for kk in range(n)
    ]
    far = [
        plan.send(windows[0, kk][:pair_rows], lambda z, x, h: (z - 1 + 2 * x, x, h))
        for kk in range(n)
    ]
    packed = pack_keys(plan, scal, k, v)
    pairs = [packed[0]]
    for kk in range(1, n):
        pairs.append(plan.partner(packed[kk], 0, kk))
    for kk in range(n):
        pairs.append(plan.partner(packed[n + kk], 1, kk))
    ordered = near + [windows[0, kk] for kk in range(n)] + [windows[1, kk] for kk in range(n)] + far

    own = value_terms(plan, scal, mask, ordered, pairs)
    near_part, far_part, mine, dk = score_terms(plan, scal, mask, ordered, pairs)
    near_sum = plan.send(near_part, lambda z, x, h: (z - 1 + 2 * x, x, h))
    far_sum = plan.send(far_part, lambda z, x, h: (z + 1 - 2 * x, x, h))
    returns = pack_returns(plan, scal, mine, near_sum, far_sum, dk)
    back = [returns[0]]
    for kk in range(1, n):
        back.append(plan.partner(returns[kk], 0, kk))
    for kk in range(n):
        back.append(plan.partner(returns[n + kk], 1, kk))
    dq, dk = unpack_returns(plan, scal, back)
    few = plan.planes <= 4 and (layer_input.shape[1] // n_blk) % 128 == 0
    dw = (weight_gradient if few else weight_gradient_summed)(plan, scal, layer_input, own)
    return jnp.moveaxis(dq, 0, 1), jnp.moveaxis(dk, 0, 1), dw


def solution(mesh):
    rows = P(AXES, None)
    cube = P(AXES, None, None)
    return jax.shard_map(
        functools.partial(local, mesh.shape["blk"], mesh.shape["head"]),
        mesh=mesh,
        in_specs=(rows, cube, cube, cube, cube, cube, rows, P()),
        out_specs=(cube, cube, P("blk", "head")),
        check_vma=False,
    )
```

```python
import functools
import math

import jax
import jax.numpy as jnp
from jax import lax
from jax.experimental import pallas as pl
from jax.experimental.pallas import tpu as pltpu
from jax.sharding import PartitionSpec as P

AXES = ("blk", "head")
STAT_ROWS = 32
MASKED = 1e30
KERNEL_VMEM = 24 * 2**20
F32 = jnp.float32
BF16 = jnp.bfloat16
VM = pl.BlockSpec(memory_space=pltpu.VMEM)
SM = pl.BlockSpec(memory_space=pltpu.SMEM)


def call(kernel, args, outs, scratch=(), flops=0, smem=1):
    moved = sum(a.size * a.dtype.itemsize for a in args) + sum(
        math.prod(o.shape) * o.dtype.itemsize for o in outs
    )
    return pl.pallas_call(
        kernel,
        out_shape=tuple(outs),
        in_specs=[SM] * smem + [VM] * (len(args) - smem),
        out_specs=tuple(VM for _ in outs),
        scratch_shapes=list(scratch),
        cost_estimate=pl.CostEstimate(flops=flops, bytes_accessed=moved, transcendentals=0),
        compiler_params=pltpu.CompilerParams(vmem_limit_bytes=KERNEL_VMEM),
    )(*args)


class Plan:
    def __init__(self, n_blk, n_head, group, block, dim):
        self.n_blk, self.n_head = n_blk, n_head
        self.planes = n_blk // 2
        self.group, self.half, self.slots = group, group // 2, group // 2 + 1
        self.block, self.dim = block, dim
        self.span = block * n_head
        self.units = [(s, 0) for s in range(self.slots)] + [(s, 1) for s in range(self.half)]

    def perm(self, move):
        pairs = []
        for z in range(self.planes):
            for x in range(2):
                for h in range(self.n_head):
                    target = move(z, x, h)
                    if target is not None and 0 <= target[0] < self.planes:
                        tz, tx, th = target
                        pairs.append(
                            ((2 * z + x) * self.n_head + h, (2 * tz + tx) * self.n_head + th)
                        )
        return pairs

    def send(self, value, move):
        return lax.ppermute(value, AXES, self.perm(move))

    def partner(self, value, i, k):
        return self.send(value, lambda z, x, h: (z, x ^ i, h ^ k))

    def head_of(self, x, slot):
        if slot == self.half:
            return self.half
        return (self.half + 1) * x + slot


def pack_queries(plan, scal, q, g, a, lse):
    group, slots, block, dim = plan.group, plan.slots, plan.block, plan.dim
    heads = q.shape[0]
    log2e = 1.0 / math.log(2.0)

    def kernel(scal_ref, q_ref, g_ref, a_ref, lse_ref, *rest):
        outs, parts = rest[:-1], rest[-1]
        x, h = scal_ref[1], scal_ref[2]
        delta = jnp.sum(g_ref[...].astype(F32) * a_ref[...].astype(F32), axis=2)
        for t, stat in enumerate((lse_ref[...] * log2e, delta)):
            high = stat.astype(BF16).astype(F32)
            rest_ = stat - high
            mid = rest_.astype(BF16).astype(F32)
            parts[t * 3, :, :] = high
            parts[t * 3 + 1, :, :] = mid
            parts[t * 3 + 2, :, :] = rest_ - mid
        pad = jnp.zeros((STAT_ROWS - 6 * slots, block), F32)
        for i in range(2):
            for k in range(plan.n_head):
                out = outs[i * plan.n_head + k]
                base = (h ^ k) * group
                rows = []
                for s in range(slots):
                    head = base + plan.head_of(x ^ i, s)
                    start = STAT_ROWS + s * 2 * block
                    out[start : start + block, :] = q_ref[head]
                    out[start + block : start + 2 * block, :] = g_ref[head]
                    rows += [parts[t, pl.ds(head, 1), :] for t in range(6)]
                out[0:STAT_ROWS, :] = jnp.concatenate(rows + [pad], axis=0).astype(BF16)

    shape = jax.ShapeDtypeStruct((STAT_ROWS + slots * 2 * block, dim), BF16)
    return call(
        kernel,
        (scal, q, g, a, lse),
        [shape] * (2 * plan.n_head),
        [pltpu.VMEM((6, heads, block), F32)],
    )


def pack_keys(plan, scal, key, val):
    group, half, slots, block, dim = plan.group, plan.half, plan.slots, plan.block, plan.dim
    n = plan.n_head

    def kernel(scal_ref, k_ref, v_ref, *outs):
        x, h = scal_ref[1], scal_ref[2]
        for i in range(2):
            for k in range(n):
                out = outs[i * n + k]
                for s in range(slots if i == 0 else half):
                    head = (h ^ k) * group + plan.head_of(x ^ i, s)
                    out[2 * s] = k_ref[head]
                    out[2 * s + 1] = v_ref[head]

    own = [jax.ShapeDtypeStruct((2 * slots, block, dim), BF16)] * n
    other = [jax.ShapeDtypeStruct((2 * half, block, dim), BF16)] * n
    return call(kernel, (scal, key, val), own + other)


def pieces_of(plan, refs, spans):
    n, found = plan.n_head, []
    refs = list(refs)
    for index, r in enumerate(spans):
        for k in range(n):
            if r in (1, 2):
                ref, first = refs.pop(0), 0
            else:
                ref = refs.pop(0) if k % 2 == 0 else ref
                first = (k % 2) * (ref.shape[0] // 2)
            found.append((index, k, ref, first, plan.half if r == 3 else plan.slots))
    return found


def gather_queries(plan, c, refs, spans, slots, q_s, g_s, lse_s, delta_s):
    block = plan.block
    for r, k, ref, first, held in pieces_of(plan, refs, spans):
        rows = pl.ds(pl.multiple_of((k ^ c) * block, block), block)
        stats = ref[first : first + STAT_ROWS, :].astype(F32)
        for s in range(min(held, slots)):
            start = first + STAT_ROWS + s * 2 * block
            w = s * len(spans) + r
            q_s[w, rows, :] = ref[start : start + block, :]
            g_s[w, rows, :] = ref[start + block : start + 2 * block, :]
            at = [stats[s * 6 + t : s * 6 + t + 1, :] for t in range(6)]
            lse_s[w, :, rows] = at[0] + (at[1] + at[2])
            delta_s[w, :, rows] = at[3] + (at[4] + at[5])


def gather_keys(plan, c, refs, which, out):
    n, block = plan.n_head, plan.block
    for u, (s, r) in enumerate(plan.units):
        for k in range(n):
            rows = pl.ds(pl.multiple_of((k ^ c) * block, block), block)
            out[u, rows, :] = refs[r * n + k][2 * s + which]


NT = (((1,), (1,)), ((), ()))


def unit_of(plan, u):
    late = (u >= plan.slots).astype(jnp.int32)
    return u - plan.slots * late, late


def weights_of(plan, mask_ref, scores, lse_row, rq, rk, half_span, scale):
    n, block = plan.n_head, plan.block
    per = n // 2
    pieces = []
    for pk in range(n):
        bias = jnp.concatenate(
            [
                jnp.full(
                    (1, block),
                    mask_ref[((rq * n + half_span * per + p) * 2 + rk) * n + pk],
                    F32,
                )
                for p in range(per)
            ],
            axis=1,
        )
        pieces.append(
            jnp.exp2(scores[pk * block : (pk + 1) * block, :] * scale - (lse_row + bias))
        )
    return jnp.concatenate(pieces, axis=0)


def value_terms(plan, scal, mask, windows, keys):
    n, dim, span = plan.n_head, plan.dim, plan.span
    nu = len(plan.units)
    scale = dim**-0.5 / math.log(2.0)
    half_rows = span // 2

    def kernel(scal_ref, mask_ref, *rest):
        c = scal_ref[3]
        q_refs, k_refs = rest[: 3 * n], rest[3 * n : 5 * n]
        out, q_s, g_s, lse_s, delta_s, k_s = rest[5 * n :]
        gather_queries(plan, c, q_refs, range(4), plan.slots, q_s, g_s, lse_s, delta_s)
        gather_keys(plan, c, k_refs, 0, k_s)

        def body(u, carry):
            slot, rk = unit_of(plan, u)
            kb = k_s[u]
            total = jnp.zeros((span, dim), F32)
            for j in range(6):
                rq = rk + j // 2
                rows = slice((j % 2) * half_rows, (j % 2 + 1) * half_rows)
                qb = q_s[slot * 4 + rq, rows, :]
                gb = g_s[slot * 4 + rq, rows, :]
                scores = lax.dot_general(kb, qb, NT, preferred_element_type=F32)
                w = weights_of(
                    plan, mask_ref, scores, lse_s[slot * 4 + rq, :, rows], rq, rk, j % 2, scale
                )
                total += jnp.dot(w.astype(BF16), gb, preferred_element_type=F32)
            out[u] = total.T.astype(BF16)
            return carry

        lax.fori_loop(0, nu, body, 0)

    return call(
        kernel,
        (scal, mask, *windows, *keys),
        [jax.ShapeDtypeStruct((nu, dim, span), BF16)],
        [
            pltpu.VMEM((plan.slots * 4, span, dim), BF16),
            pltpu.VMEM((plan.slots * 4, span, dim), BF16),
            pltpu.VMEM((plan.slots * 4, 1, span), F32),
            pltpu.VMEM((plan.slots * 4, 1, span), F32),
            pltpu.VMEM((nu, span, dim), BF16),
        ],
        flops=nu * 2 * 2 * 3 * span * span * dim,
        smem=2,
    )[0]


def score_terms(plan, scal, mask, windows, keys, rk):
    n, block, dim, span = plan.n_head, plan.block, plan.dim, plan.span
    slots = plan.half if rk else plan.slots
    score_scale = dim**-0.5
    scale = score_scale / math.log(2.0)
    half_rows = span // 2
    count = len(windows)
    spans = range(rk, rk + 3)
    outer, inner = (2, (0, 1)) if rk else (0, (1, 2))

    def kernel(scal_ref, mask_ref, *rest):
        c = scal_ref[3]
        q_refs, k_refs = rest[:count], rest[count : count + n]
        out, mine, dk_out, q_s, g_s, lse_s, delta_s, k_s, v_s, dq_s = rest[count + n :]
        gather_queries(plan, c, q_refs, spans, slots, q_s, g_s, lse_s, delta_s)
        for k in range(n):
            rows = pl.ds(pl.multiple_of((k ^ c) * block, block), block)
            for s in range(slots):
                k_s[s, rows, :] = k_refs[k][2 * s]
                v_s[s, rows, :] = k_refs[k][2 * s + 1]

        def body(s, carry):
            kb = k_s[s]
            vb = v_s[s]
            kt = kb.T
            total = jnp.zeros((span, dim), F32)
            for j in range(6):
                at = s * 3 + j // 2
                rows = slice((j % 2) * half_rows, (j % 2 + 1) * half_rows)
                qb = q_s[at, rows, :]
                gb = g_s[at, rows, :]
                scores = lax.dot_general(kb, qb, NT, preferred_element_type=F32)
                w = weights_of(
                    plan, mask_ref, scores, lse_s[at, :, rows], rk + j // 2, rk, j % 2, scale
                )
                dw = lax.dot_general(vb, gb, NT, preferred_element_type=F32)
                ds = (w * (dw - delta_s[at, :, rows])).astype(BF16)
                total += jnp.dot(ds, qb, preferred_element_type=F32)
                dq_s[at, :, rows] = jnp.dot(kt, ds, preferred_element_type=F32)
            dk_out[s] = (total * score_scale).astype(BF16)
            return carry

        lax.fori_loop(0, slots, body, 0)
        for s in range(slots):
            out[s] = (dq_s[s * 3 + outer].T * score_scale).astype(BF16)
            for i, r in enumerate(inner):
                mine[i * slots + s] = dq_s[s * 3 + r].T * score_scale

    return call(
        kernel,
        (scal, mask, *windows, *keys),
        [
            jax.ShapeDtypeStruct((slots, span, dim), BF16),
            jax.ShapeDtypeStruct((2 * slots, span, dim), F32),
            jax.ShapeDtypeStruct((slots, span, dim), BF16),
        ],
        [
            pltpu.VMEM((slots * 3, span, dim), BF16),
            pltpu.VMEM((slots * 3, span, dim), BF16),
            pltpu.VMEM((slots * 3, 1, span), F32),
            pltpu.VMEM((slots * 3, 1, span), F32),
            pltpu.VMEM((slots, span, dim), BF16),
            pltpu.VMEM((slots, span, dim), BF16),
            pltpu.VMEM((slots * 3, dim, span), F32),
        ],
        flops=slots * 4 * 2 * 3 * span * span * dim,
        smem=2,
    )


def pack_returns(plan, scal, near, far, mine, dk):
    block, dim, slots, half = plan.block, plan.dim, plan.slots, plan.half

    def kernel(scal_ref, near_ref, far_ref, mine0, mine1, dk0, dk1, *outs):
        c = scal_ref[3]
        for i in range(2):
            for k in range(plan.n_head):
                out = outs[i * plan.n_head + k]
                rows = pl.ds(pl.multiple_of((k ^ c) * block, block), block)
                for s in range(slots):
                    total = mine0[i * slots + s, rows, :]
                    if s < half:
                        total += mine1[i * half + s, rows, :]
                    if i == 1:
                        total += near_ref[s, rows, :].astype(F32)
                    elif s < half:
                        total += far_ref[s, rows, :].astype(F32)
                    out[s] = total.astype(BF16)
                for s in range(slots if i == 0 else half):
                    out[slots + s] = (dk1 if i else dk0)[s, rows, :]

    own = jax.ShapeDtypeStruct((2 * slots, block, dim), BF16)
    other = jax.ShapeDtypeStruct((slots + half, block, dim), BF16)
    return call(kernel, (scal, near, far, *mine, *dk), [own] * plan.n_head + [other] * plan.n_head)


def unpack_returns(plan, scal, bufs):
    block, dim, slots, half, n = plan.block, plan.dim, plan.slots, plan.half, plan.n_head
    heads = n * plan.group

    def kernel(scal_ref, *rest):
        refs, (dq, dk) = rest[: 2 * n], rest[2 * n :]
        x, h = scal_ref[1], scal_ref[2]
        for k in range(n):
            base = (h ^ k) * plan.group
            for i in range(2):
                ref = refs[i * n + k]
                for s in range(half):
                    head = base + plan.head_of(x ^ i, s)
                    dq[head] = ref[s]
                    dk[head] = ref[slots + s]
            both = refs[k][half].astype(F32) + refs[n + k][half].astype(F32)
            dq[base + half] = both.astype(BF16)
            dk[base + half] = refs[k][slots + half]

    shape = jax.ShapeDtypeStruct((heads, block, dim), BF16)
    return call(kernel, (scal, *bufs), [shape, shape])


def split_rows(plan, scal, rows):
    tokens, width = rows.shape
    cols = width // plan.planes

    def kernel(scal_ref, in_ref, *outs):
        for k, out in enumerate(outs):
            plane = lax.rem(scal_ref[0] + k, plan.planes)
            out[...] = in_ref[:, pl.ds(pl.multiple_of(plane * cols, cols), cols)]

    shape = jax.ShapeDtypeStruct((tokens, cols), BF16)
    return call(kernel, (scal, rows), [shape] * plan.planes)


def spread_rows(plan, scal, rows):
    pieces = [
        plan.send(piece, lambda z, x, h, k=k: ((z + k) % plan.planes, x, h))
        if k
        else piece
        for k, piece in enumerate(split_rows(plan, scal, rows))
    ]
    cols = pieces[0].shape[1] // 2
    even = scal[3] == 0
    out = []
    size = max(plan.planes // 2, 1)
    for batch in range(0, plan.planes, size):
        part = pieces[batch : batch + size]
        mine = [jnp.where(even, p[:, :cols], p[:, cols:]) for p in part]
        others = jnp.stack([jnp.where(even, p[:, cols:], p[:, :cols]) for p in part])
        crossed = plan.partner(others, 0, 1)
        base = jnp.stack(
            [
                jnp.concatenate(
                    (
                        jnp.where(even, mine[k], crossed[k]),
                        jnp.where(even, crossed[k], mine[k]),
                    )
                )
                for k in range(size)
            ]
        )
        by_x = plan.partner(base, 1, 0)
        by_y = plan.partner(base, 0, 2)
        if batch == 0:
            both = plan.partner(by_x, 0, 2)
        else:
            both = plan.partner(by_y, 1, 0)
        out += [((base, by_y, by_x, both), at) for at in range(size)]
    return out


def weight_terms(plan, scal, totals, steps, only=None):
    depth, cols = steps[0][0][0][0].shape[1:]
    span, dim, slots = plan.span, plan.dim, plan.slots
    nu = len(plan.units)
    wide, pair = slots * dim, (nu - slots) * dim
    halves = range(2) if only is None else (only,)
    first = totals is None
    args, specs, steps_at = [], [], []
    for (flat, place), terms in steps:
        steps_at.append(len(args))
        args += [*flat, *terms]
        specs += [pl.BlockSpec((1, depth, cols), lambda g, place=place: (place, 0, 0))] * 4
        specs += [VM, VM]
    totals_at = len(args)
    if not first:
        args += [totals[at] for at in halves]
        specs += [VM] * len(halves)

    def kernel(scal_ref, *rest):
        flip = scal_ref[1] ^ scal_ref[3]
        outs = rest[len(args) :]

        def left(l, lo, hi):
            return [rest[base + 4 + l][lo:hi].reshape((hi - lo) * dim, span) for base in steps_at]

        def right(i):
            return [
                jnp.concatenate([rest[base + 2 * i + j][0] for j in range(2)]) for base in steps_at
            ]

        def write(l, slot):
            half = nu - slots
            pairs = jnp.concatenate(left(l, 0, half) + left(l, slots, nu), axis=1)
            middle = jnp.concatenate(left(l, half, slots), axis=1)
            own, other = right(0), right(1)
            for value, rows in (
                (
                    jnp.dot(pairs, jnp.concatenate(own + other), preferred_element_type=F32),
                    slice(0, pair),
                ),
                (
                    jnp.dot(middle, jnp.concatenate(own), preferred_element_type=F32),
                    slice(pair, wide),
                ),
            ):
                if not first:
                    value += rest[totals_at + slot][rows, :]
                outs[slot][rows, :] = value.astype(outs[slot].dtype)

        for slot, at in enumerate(halves):
            for l in range(2):

                @pl.when(flip == (at ^ l))
                def _(l=l, slot=slot):
                    write(l, slot)

    out = jax.ShapeDtypeStruct((wide, cols), F32 if only is None else BF16)
    flops = 2 * nu * dim * span * cols * len(steps) * len(halves)
    return pl.pallas_call(
        kernel,
        out_shape=(out,) * len(halves),
        grid=(1,),
        in_specs=[SM] + specs,
        out_specs=(VM,) * len(halves),
        cost_estimate=pl.CostEstimate(
            flops=flops, bytes_accessed=wide * cols * 8 + 6 * span * cols, transcendentals=0
        ),
        compiler_params=pltpu.CompilerParams(vmem_limit_bytes=KERNEL_VMEM),
    )(scal, *args)


def finish_weights(plan, scal, near, far):
    _, cols = near.shape
    pair, dim = plan.half * plan.dim, plan.dim

    def kernel(scal_ref, near_ref, far_ref, out):
        c = scal_ref[3]

        def write(low, high):
            out[:, 0:pair] = low[0:pair, :].T.astype(F32)
            out[:, pair + dim :] = high[0:pair, :].T.astype(F32)
            middle = low[pair:, :].T.astype(F32) + high[pair:, :].T.astype(F32)
            out[:, pair : pair + dim] = middle

        @pl.when(c == 0)
        def _():
            write(near_ref, far_ref)

        @pl.when(c == 1)
        def _():
            write(far_ref, near_ref)

    return call(kernel, (scal, near, far), [jax.ShapeDtypeStruct((cols, 2 * pair + dim), F32)])[0]


def weight_gradient(plan, scal, rows, own):
    steps = []
    value = own
    for k, pieces in enumerate(spread_rows(plan, scal, rows)):
        if k:
            value = plan.send(value, lambda z, x, h: ((z + 1) % plan.planes, x, h))
        steps.append((pieces, (value, plan.partner(value, 0, 1))))
    total = None
    for index in range(0, len(steps) - 1, 2):
        part = steps[index : min(index + 2, len(steps) - 1)]
        total = weight_terms(plan, scal, total, part)
    (near,) = weight_terms(plan, scal, total, steps[-1:], 0)
    (far,) = weight_terms(plan, scal, total, steps[-1:], 1)
    near = plan.send(near, lambda z, x, h: (z, h & 1, (h & ~1) | x))
    far = plan.send(far, lambda z, x, h: (z, h & 1, (h & ~1) | (x ^ 1)))
    return finish_weights(plan, scal, near, far)


def weight_gradient_summed(plan, scal, rows, own):
    h, x = scal[2], scal[1]
    half, slots, dim, span = plan.half, plan.slots, plan.dim, plan.span
    other = plan.partner(own[slots:], 1, 0)
    low = jnp.where(x == 0, own[:half], other)
    high = jnp.where(x == 0, other, own[:half])
    value = jnp.concatenate([low, own[half:slots], high], axis=0)
    value = value.reshape(plan.group * dim, plan.n_head, plan.block)
    places = jnp.arange(plan.n_head, dtype=jnp.int32) ^ (h & ~1)
    value = jnp.take(value, places, axis=1).reshape(plan.group * dim, span)
    gathered = lax.all_gather(rows, "head", axis=0, tiled=True)
    product = jnp.einsum("ts,ct->sc", gathered, value, preferred_element_type=F32)
    return lax.psum_scatter(product, "blk", scatter_dimension=0, tiled=True)


def local(n_blk, n_head, layer_input, queries, keys, values, out_grad, attn_out, log_sum, blocks):
    tokens, heads, dim = queries.shape
    plan = Plan(n_blk, n_head, heads // n_head, tokens, dim)
    n = n_head
    b, h = lax.axis_index("blk"), lax.axis_index("head")
    z, x, c = b // 2, b % 2, h % 2
    scal = jnp.stack([z, x, h, c]).astype(jnp.int32)
    z, x, h, c = scal[0], scal[1], scal[2], scal[3]
    by_head = lambda v: jnp.moveaxis(v, 1, 0)
    q, g, a, k, v = (by_head(m) for m in (queries, out_grad, attn_out, keys, values))

    places = jnp.arange(n, dtype=jnp.int32) ^ (h & ~1)
    spans = b + (1 - 2 * x) * jnp.arange(-1, 3, dtype=jnp.int32)
    query_ids = (spans[:, None] * n + places[None, :]).reshape(-1)
    key_ids = (spans[1:3, None] * n + places[None, :]).reshape(-1)
    inside = (query_ids >= 0) & (query_ids < blocks.shape[0])
    listed = blocks[jnp.where(inside, query_ids, 0)]
    linked = jnp.any(listed[:, None, :] == key_ids[None, :, None], axis=2) & inside[:, None]
    mask = jnp.where(linked, 0.0, MASKED).astype(F32).reshape(-1)

    sent = pack_queries(plan, scal, q, g, a, log_sum.T)
    windows = {(0, 0): sent[0]}
    for i, kk in [(1, kk) for kk in range(n)] + [(0, kk) for kk in range(1, n)]:
        windows[i, kk] = plan.partner(sent[i * n + kk], i, kk)
    pair_rows = STAT_ROWS + plan.half * 2 * tokens
    outward = lambda z, x, h: (z + 1 - 2 * x, x, h)
    inward = lambda z, x, h: (z - 1 + 2 * x, x, h)
    pairs = [(kk, kk + 1) for kk in range(0, n, 2)]


    def join(i, rows, kks):
        return jnp.concatenate([windows[i, kk][:rows] for kk in kks])

    all_rows = sent[0].shape[0]
    near = [plan.send(join(1, all_rows, kk), outward) for kk in pairs]
    far = [plan.send(join(0, pair_rows, kk), inward) for kk in pairs]
    packed = pack_keys(plan, scal, k, v)
    moved = [packed[0]]
    moved += [plan.partner(packed[kk], 0, kk) for kk in range(1, n)]
    moved += [plan.partner(packed[n + kk], 1, kk) for kk in range(n)]
    ordered = near + [windows[0, kk] for kk in range(n)] + [windows[1, kk] for kk in range(n)] + far

    own = value_terms(plan, scal, mask, ordered, moved)
    inner = [windows[i, kk] for i in range(2) for kk in range(n)]
    near_part, mine0, dk0 = score_terms(plan, scal, mask, near + inner, moved[:n], 0)
    far_part, mine1, dk1 = score_terms(plan, scal, mask, inner + far, moved[n:], 1)
    near_sum = plan.send(near_part, inward)
    far_sum = plan.send(far_part, outward)
    returns = pack_returns(plan, scal, near_sum, far_sum, (mine0, mine1), (dk0, dk1))
    back = [returns[0]]
    back += [plan.partner(returns[kk], 0, kk) for kk in range(1, n)]
    back += [plan.partner(returns[n + kk], 1, kk) for kk in range(n)]
    dq, dk = unpack_returns(plan, scal, back)
    few = plan.planes <= 4 and (layer_input.shape[1] // n_blk) % 128 == 0
    dw = (weight_gradient if few else weight_gradient_summed)(plan, scal, layer_input, own)
    return jnp.moveaxis(dq, 0, 1), jnp.moveaxis(dk, 0, 1), dw


def solution(mesh):
    rows = P(AXES, None)
    cube = P(AXES, None, None)
    body = functools.partial(local, mesh.shape["blk"], mesh.shape["head"])
    return jax.shard_map(
        body,
        mesh=mesh,
        in_specs=(rows, cube, cube, cube, cube, cube, rows, P()),
        out_specs=(cube, cube, P("blk", "head")),
        check_vma=False,
    )
```

```python
import functools
import math

import jax
import jax.numpy as jnp
from jax import lax
from jax.experimental import pallas as pl
from jax.experimental.pallas import tpu as pltpu
from jax.sharding import PartitionSpec as P

AXES = ("blk", "head")
STAT_ROWS = 32
MASKED = 1e30
KERNEL_VMEM = 14 * 2**20
F32 = jnp.float32
BF16 = jnp.bfloat16
VM = pl.BlockSpec(memory_space=pltpu.VMEM)
SM = pl.BlockSpec(memory_space=pltpu.SMEM)


def call(kernel, args, outs, scratch=(), flops=0, smem=1):
    moved = sum(a.size * a.dtype.itemsize for a in args) + sum(
        math.prod(o.shape) * o.dtype.itemsize for o in outs
    )
    return pl.pallas_call(
        kernel,
        out_shape=tuple(outs),
        in_specs=[SM] * smem + [VM] * (len(args) - smem),
        out_specs=tuple(VM for _ in outs),
        scratch_shapes=list(scratch),
        cost_estimate=pl.CostEstimate(flops=flops, bytes_accessed=moved, transcendentals=0),
        compiler_params=pltpu.CompilerParams(vmem_limit_bytes=KERNEL_VMEM),
    )(*args)


class Plan:
    def __init__(self, n_blk, n_head, group, block, dim):
        self.n_blk, self.n_head = n_blk, n_head
        self.planes = n_blk // 2
        self.group, self.half, self.slots = group, group // 2, group // 2 + 1
        self.block, self.dim = block, dim
        self.span = block * n_head
        self.groups = ((0, self.half), tuple(range(1, self.half)))

    def perm(self, move):
        pairs = []
        for z in range(self.planes):
            for x in range(2):
                for h in range(self.n_head):
                    target = move(z, x, h)
                    if target is not None and 0 <= target[0] < self.planes:
                        tz, tx, th = target
                        pairs.append(
                            ((2 * z + x) * self.n_head + h, (2 * tz + tx) * self.n_head + th)
                        )
        return pairs

    def send(self, value, move):
        return lax.ppermute(value, AXES, self.perm(move))

    def partner(self, value, i, k):
        return self.send(value, lambda z, x, h: (z, x ^ i, h ^ k))

    def head_of(self, x, slot):
        if slot == self.half:
            return self.half
        return (self.half + 1) * x + slot


def pack_queries(plan, scal, q, g, a, lse):
    group, slots, block, dim = plan.group, plan.slots, plan.block, plan.dim
    heads = q.shape[0]
    log2e = 1.0 / math.log(2.0)

    def kernel(scal_ref, q_ref, g_ref, a_ref, lse_ref, *rest):
        outs, parts = rest[:-1], rest[-1]
        x, h = scal_ref[1], scal_ref[2]
        delta = jnp.sum(g_ref[...].astype(F32) * a_ref[...].astype(F32), axis=2)
        for t, stat in enumerate((lse_ref[...] * log2e, delta)):
            high = stat.astype(BF16).astype(F32)
            rest_ = stat - high
            mid = rest_.astype(BF16).astype(F32)
            parts[t * 3, :, :] = high
            parts[t * 3 + 1, :, :] = mid
            parts[t * 3 + 2, :, :] = rest_ - mid
        pad = jnp.zeros((STAT_ROWS - 6 * slots, block), F32)
        for i in range(2):
            for k in range(plan.n_head):
                out = outs[i * plan.n_head + k]
                base = (h ^ k) * group
                rows = []
                for s in range(slots):
                    head = base + plan.head_of(x ^ i, s)
                    start = STAT_ROWS + s * 2 * block
                    out[start : start + block, :] = q_ref[head]
                    out[start + block : start + 2 * block, :] = g_ref[head]
                    rows += [parts[t, pl.ds(head, 1), :] for t in range(6)]
                out[0:STAT_ROWS, :] = jnp.concatenate(rows + [pad], axis=0).astype(BF16)

    shape = jax.ShapeDtypeStruct((STAT_ROWS + slots * 2 * block, dim), BF16)
    return call(
        kernel,
        (scal, q, g, a, lse),
        [shape] * (2 * plan.n_head),
        [pltpu.VMEM((6, heads, block), F32)],
    )


def pack_keys(plan, scal, key, val):
    group, half, slots, block, dim = plan.group, plan.half, plan.slots, plan.block, plan.dim
    n = plan.n_head

    def kernel(scal_ref, k_ref, v_ref, *outs):
        x, h = scal_ref[1], scal_ref[2]
        for i in range(2):
            for k in range(n):
                out = outs[i * n + k]
                for s in range(slots if i == 0 else half):
                    head = (h ^ k) * group + plan.head_of(x ^ i, s)
                    out[2 * s] = k_ref[head]
                    out[2 * s + 1] = v_ref[head]

    own = [jax.ShapeDtypeStruct((2 * slots, block, dim), BF16)] * n
    other = [jax.ShapeDtypeStruct((2 * half, block, dim), BF16)] * n
    return call(kernel, (scal, key, val), own + other)


def link_mask(plan, scal, blocks):
    n, total, listed = plan.n_head, blocks.shape[0], blocks.shape[1]

    def kernel(scal_ref, list_ref, out):
        z, x, h = scal_ref[0], scal_ref[1], scal_ref[2]
        sign = 1 - 2 * x
        base = h & ~1
        keys = [(2 * z + x + sign * r) * n + (p ^ base) for r in range(2) for p in range(n)]

        def body(index, carry):
            query = (2 * z + x + sign * (index // n - 1)) * n + (lax.rem(index, n) ^ base)
            inside = (query >= 0) & (query < total)
            row = jnp.where(inside, query, 0) * listed
            entries = [list_ref[row + s] for s in range(listed)]
            for m, key in enumerate(keys):
                found = entries[0] == key
                for entry in entries[1:]:
                    found = found | (entry == key)
                out[index * 2 * n + m] = jnp.where(found & inside, 0.0, MASKED).astype(F32)
            return carry

        lax.fori_loop(0, 4 * n, body, 0)

    return pl.pallas_call(
        kernel,
        name="km",
        out_shape=jax.ShapeDtypeStruct((8 * n * n,), F32),
        in_specs=[SM, SM],
        out_specs=SM,
        cost_estimate=pl.CostEstimate(flops=0, bytes_accessed=4 * blocks.size, transcendentals=0),
        compiler_params=pltpu.CompilerParams(vmem_limit_bytes=KERNEL_VMEM),
    )(scal, blocks.reshape(-1))


def pieces_of(plan, refs, spans):
    n, found = plan.n_head, []
    refs = list(refs)
    for index, r in enumerate(spans):
        for k in range(n):
            if r in (1, 2):
                ref, first = refs.pop(0), 0
            else:
                ref = refs.pop(0) if k % 2 == 0 else ref
                first = (k % 2) * (ref.shape[0] // 2)
            found.append((index, k, ref, first, plan.half if r == 3 else plan.slots))
    return found


def gather_queries(plan, c, refs, spans, slots, q_s, g_s, lse_s, delta_s):
    block = plan.block
    for r, k, ref, first, held in pieces_of(plan, refs, spans):
        rows = pl.ds(pl.multiple_of((k ^ c) * block, block), block)
        stats = ref[first : first + STAT_ROWS, :].astype(F32)
        for i, s in enumerate(slots):
            if s >= held:
                continue
            start = first + STAT_ROWS + s * 2 * block
            w = i * len(spans) + r
            q_s[w, rows, :] = ref[start : start + block, :]
            g_s[w, rows, :] = ref[start + block : start + 2 * block, :]
            at = [stats[s * 6 + t : s * 6 + t + 1, :] for t in range(6)]
            lse_s[w, :, rows] = at[0] + (at[1] + at[2])
            delta_s[w, :, rows] = at[3] + (at[4] + at[5])


NT = (((1,), (1,)), ((), ()))


def weights_of(plan, mask_ref, scores, lse_row, rq, rk, half_span, scale):
    n, block = plan.n_head, plan.block
    per = n // 2
    pieces = []
    for pk in range(n):
        bias = jnp.concatenate(
            [
                jnp.full(
                    (1, block),
                    mask_ref[((rq * n + half_span * per + p) * 2 + rk) * n + pk],
                    F32,
                )
                for p in range(per)
            ],
            axis=1,
        )
        pieces.append(
            jnp.exp2(scores[pk * block : (pk + 1) * block, :] * scale - (lse_row + bias))
        )
    return jnp.concatenate(pieces, axis=0)


def value_terms(plan, scal, mask, windows, keys, group):
    n, block, dim, span = plan.n_head, plan.block, plan.dim, plan.span
    slots = plan.groups[group]
    units = [(i, s, 0) for i, s in enumerate(slots)]
    units += [(i, s, 1) for i, s in enumerate(slots) if s < plan.half]
    nu = len(units)
    scale = dim**-0.5 / math.log(2.0)
    half_rows = span // 2

    def kernel(scal_ref, mask_ref, *rest):
        c = scal_ref[3]
        q_refs, k_refs = rest[: 3 * n], rest[3 * n : 5 * n]
        out, q_s, g_s, lse_s, delta_s, k_s = rest[5 * n :]
        gather_queries(plan, c, q_refs, range(4), slots, q_s, g_s, lse_s, delta_s)
        for u, (_, s, r) in enumerate(units):
            for k in range(n):
                rows = pl.ds(pl.multiple_of((k ^ c) * block, block), block)
                k_s[u, rows, :] = k_refs[r * n + k][2 * s]

        def body(u, carry):
            rk = (u >= len(slots)).astype(jnp.int32)
            first = (u - len(slots) * rk) * 4 + rk
            kb = k_s[u]
            total = jnp.zeros((span, dim), F32)
            for j in range(6):
                rows = slice((j % 2) * half_rows, (j % 2 + 1) * half_rows)
                at = first + j // 2
                qb = q_s[at, rows, :]
                gb = g_s[at, rows, :]
                scores = lax.dot_general(kb, qb, NT, preferred_element_type=F32)
                w = weights_of(
                    plan, mask_ref, scores, lse_s[at, :, rows], rk + j // 2, rk, j % 2, scale
                )
                total += jnp.dot(w.astype(BF16), gb, preferred_element_type=F32)
            out[u] = total.T.astype(BF16)
            return carry

        lax.fori_loop(0, nu, body, 0)

    held = len(slots) * 4
    return call(
        kernel,
        (scal, mask, *windows, *keys),
        [jax.ShapeDtypeStruct((nu, dim, span), BF16)],
        [
            pltpu.VMEM((held, span, dim), BF16),
            pltpu.VMEM((held, span, dim), BF16),
            pltpu.VMEM((held, 1, span), F32),
            pltpu.VMEM((held, 1, span), F32),
            pltpu.VMEM((nu, span, dim), BF16),
        ],
        flops=nu * 2 * 2 * 3 * span * span * dim,
        smem=2,
    )[0]


def score_terms(plan, scal, mask, windows, keys, rk):
    n, block, dim, span = plan.n_head, plan.block, plan.dim, plan.span
    slots = plan.half if rk else plan.slots
    score_scale = dim**-0.5
    scale = score_scale / math.log(2.0)
    half_rows = span // 2
    count = len(windows)
    spans = range(rk, rk + 3)
    outer, inner = (2, (0, 1)) if rk else (0, (1, 2))

    def kernel(scal_ref, mask_ref, *rest):
        c = scal_ref[3]
        q_refs, k_refs = rest[:count], rest[count : count + n]
        out, mine, dk_out, q_s, g_s, lse_s, delta_s, k_s, v_s, dq_s = rest[count + n :]
        gather_queries(plan, c, q_refs, spans, range(slots), q_s, g_s, lse_s, delta_s)
        for k in range(n):
            rows = pl.ds(pl.multiple_of((k ^ c) * block, block), block)
            for s in range(slots):
                k_s[s, rows, :] = k_refs[k][2 * s]
                v_s[s, rows, :] = k_refs[k][2 * s + 1]

        def body(s, carry):
            kb = k_s[s]
            vb = v_s[s]
            kt = kb.T
            total = jnp.zeros((span, dim), F32)
            for j in range(6):
                at = s * 3 + j // 2
                rows = slice((j % 2) * half_rows, (j % 2 + 1) * half_rows)
                qb = q_s[at, rows, :]
                gb = g_s[at, rows, :]
                scores = lax.dot_general(kb, qb, NT, preferred_element_type=F32)
                w = weights_of(
                    plan, mask_ref, scores, lse_s[at, :, rows], rk + j // 2, rk, j % 2, scale
                )
                dw = lax.dot_general(vb, gb, NT, preferred_element_type=F32)
                ds = (w * (dw - delta_s[at, :, rows])).astype(BF16)
                total += jnp.dot(ds, qb, preferred_element_type=F32)
                dq_s[at, :, rows] = jnp.dot(kt, ds, preferred_element_type=F32)
            dk_out[s] = (total * score_scale).astype(BF16)
            return carry

        lax.fori_loop(0, slots, body, 0)
        for s in range(slots):
            out[s] = (dq_s[s * 3 + outer].T * score_scale).astype(BF16)
            for i, r in enumerate(inner):
                mine[i * slots + s] = dq_s[s * 3 + r].T * score_scale

    return call(
        kernel,
        (scal, mask, *windows, *keys),
        [
            jax.ShapeDtypeStruct((slots, span, dim), BF16),
            jax.ShapeDtypeStruct((2 * slots, span, dim), F32),
            jax.ShapeDtypeStruct((slots, span, dim), BF16),
        ],
        [
            pltpu.VMEM((slots * 3, span, dim), BF16),
            pltpu.VMEM((slots * 3, span, dim), BF16),
            pltpu.VMEM((slots * 3, 1, span), F32),
            pltpu.VMEM((slots * 3, 1, span), F32),
            pltpu.VMEM((slots, span, dim), BF16),
            pltpu.VMEM((slots, span, dim), BF16),
            pltpu.VMEM((slots * 3, dim, span), F32),
        ],
        flops=slots * 4 * 2 * 3 * span * span * dim,
        smem=2,
    )


def pack_returns(plan, scal, i, outer, mine, dk):
    block, dim, slots, half = plan.block, plan.dim, plan.slots, plan.half
    held = slots if i else half

    def kernel(scal_ref, outer_ref, mine0, mine1, dk_ref, *outs):
        c = scal_ref[3]
        for k, out in enumerate(outs):
            rows = pl.ds(pl.multiple_of((k ^ c) * block, block), block)
            for s in range(slots):
                total = mine0[i * slots + s, rows, :]
                if s < half:
                    total += mine1[i * half + s, rows, :]
                if s < held:
                    total += outer_ref[s, rows, :].astype(F32)
                out[s] = total.astype(BF16)
            for s in range(half if i else slots):
                out[slots + s] = dk_ref[s, rows, :]

    shape = jax.ShapeDtypeStruct((slots + (half if i else slots), block, dim), BF16)
    return call(kernel, (scal, outer, *mine, dk), [shape] * plan.n_head)


def unpack_returns(plan, scal, bufs):
    block, dim, slots, half, n = plan.block, plan.dim, plan.slots, plan.half, plan.n_head
    heads = n * plan.group

    def kernel(scal_ref, *rest):
        refs, (dq, dk) = rest[: 2 * n], rest[2 * n :]
        x, h = scal_ref[1], scal_ref[2]
        for k in range(n):
            base = (h ^ k) * plan.group
            for i in range(2):
                ref = refs[i * n + k]
                for s in range(half):
                    head = base + plan.head_of(x ^ i, s)
                    dq[head] = ref[s]
                    dk[head] = ref[slots + s]
            both = refs[k][half].astype(F32) + refs[n + k][half].astype(F32)
            dq[base + half] = both.astype(BF16)
            dk[base + half] = refs[k][slots + half]

    shape = jax.ShapeDtypeStruct((heads, block, dim), BF16)
    return call(kernel, (scal, *bufs), [shape, shape])


def split_rows(plan, scal, rows):
    tokens, width = rows.shape
    cols = width // plan.planes

    def kernel(scal_ref, in_ref, *outs):
        for k, out in enumerate(outs):
            plane = lax.rem(scal_ref[0] + k, plan.planes)
            out[...] = in_ref[:, pl.ds(pl.multiple_of(plane * cols, cols), cols)]

    shape = jax.ShapeDtypeStruct((tokens, cols), BF16)
    return call(kernel, (scal, rows), [shape] * plan.planes)


def spread_rows(plan, scal, rows):
    pieces = [
        plan.send(piece, lambda z, x, h, k=k: ((z + k) % plan.planes, x, h))
        if k
        else piece
        for k, piece in enumerate(split_rows(plan, scal, rows))
    ]
    cols = pieces[0].shape[1] // 2
    even = scal[3] == 0
    out = []
    size = max(plan.planes // 2, 1)
    for batch in range(0, plan.planes, size):
        part = pieces[batch : batch + size]
        mine = [jnp.where(even, p[:, :cols], p[:, cols:]) for p in part]
        others = jnp.stack([jnp.where(even, p[:, cols:], p[:, :cols]) for p in part])
        crossed = plan.partner(others, 0, 1)
        base = jnp.stack(
            [
                jnp.concatenate(
                    (
                        jnp.where(even, mine[k], crossed[k]),
                        jnp.where(even, crossed[k], mine[k]),
                    )
                )
                for k in range(size)
            ]
        )
        by_x = plan.partner(base, 1, 0)
        by_y = plan.partner(base, 0, 2)
        if batch == 0:
            both = plan.partner(by_x, 0, 2)
        else:
            both = plan.partner(by_y, 1, 0)
        out += [((base, by_y, by_x, both), at) for at in range(size)]
    return out


def weight_terms(plan, scal, totals, steps, group=None, only=None):
    depth, cols = steps[0][0][0][0].shape[1:]
    span, dim, half = plan.span, plan.dim, plan.half
    groups = (0, 1) if group is None else (group,)
    halves = range(2) if only is None else (only,)
    first = totals is None
    args, specs, steps_at = [], [], []
    for (flat, place), terms in steps:
        steps_at.append(len(args))
        args += [*flat]
        specs += [pl.BlockSpec((1, depth, cols), lambda g, place=place: (place, 0, 0))] * 4
        for m in groups:
            args += [*terms[m]]
            specs += [VM, VM]
    totals_at = len(args)
    if not first:
        args += [totals[at] for at in halves]
        specs += [VM] * len(halves)
    tops = {0: 0, 1: 2 * dim}
    sizes = {0: 2 * dim, 1: (half - 1) * dim}

    def kernel(scal_ref, *rest):
        flip = scal_ref[1] ^ scal_ref[3]
        outs = rest[len(args) :]

        def right(i):
            return [
                jnp.concatenate([rest[base + 2 * i + j][0] for j in range(2)]) for base in steps_at
            ]

        def write(l, slot):
            own, other = right(0), right(1)
            both, own = jnp.concatenate(own + other), jnp.concatenate(own)
            for index, m in enumerate(groups):
                refs = [rest[base + 4 + 2 * index + l] for base in steps_at]

                def rows_of(unit):
                    return [ref[unit] for ref in refs]

                count = 1 if m == 0 else half - 1
                parts = []
                for s in range(count):
                    left = jnp.concatenate(
                        rows_of(s) + rows_of(2 if m == 0 else count + s), axis=1
                    )
                    parts.append((s * dim if m else 0, left, both))
                if m == 0:
                    parts.append((dim, jnp.concatenate(rows_of(1), axis=1), own))
                for top, left, right_ in parts:
                    value = jnp.dot(left, right_, preferred_element_type=F32)
                    at = tops[m] + top
                    if not first:
                        value += rest[totals_at + slot][at : at + dim, :]
                    start = top if group is not None else at
                    outs[slot][start : start + dim, :] = value.astype(outs[slot].dtype)

        for slot, at in enumerate(halves):
            for l in range(2):

                @pl.when(flip == (at ^ l))
                def _(l=l, slot=slot):
                    write(l, slot)

    wide = sum(sizes[m] for m in groups)
    out = jax.ShapeDtypeStruct((wide, cols), F32 if group is None else BF16)
    flops = 4 * wide * span * cols * len(steps) * len(halves)
    return pl.pallas_call(
        kernel,
        out_shape=(out,) * len(halves),
        grid=(1,),
        in_specs=[SM] + specs,
        out_specs=(VM,) * len(halves),
        cost_estimate=pl.CostEstimate(
            flops=flops, bytes_accessed=wide * cols * 8 + 6 * span * cols, transcendentals=0
        ),
        compiler_params=pltpu.CompilerParams(vmem_limit_bytes=KERNEL_VMEM),
    )(scal, *args)


def finish_weights(plan, scal, near, far):
    cols = near[0].shape[1]
    dim, half = plan.dim, plan.half

    def kernel(scal_ref, near0, near1, far0, far1, out):
        c = scal_ref[3]

        def write(low, high):
            for start, (first, others) in ((0, low), ((half + 1) * dim, high)):
                out[:, start : start + dim] = first[0:dim, :].T.astype(F32)
                out[:, start + dim : start + half * dim] = others[...].T.astype(F32)
            middle = low[0][dim:, :].T.astype(F32) + high[0][dim:, :].T.astype(F32)
            out[:, half * dim : (half + 1) * dim] = middle

        @pl.when(c == 0)
        def _():
            write((near0, near1), (far0, far1))

        @pl.when(c == 1)
        def _():
            write((far0, far1), (near0, near1))

    return call(
        kernel, (scal, *near, *far), [jax.ShapeDtypeStruct((cols, plan.group * dim), F32)]
    )[0]


def weight_gradient(plan, scal, rows, own):
    steps = []
    values = list(own)
    for k, pieces in enumerate(spread_rows(plan, scal, rows)):
        terms = []
        for m in range(2):
            if k:
                values[m] = plan.send(values[m], lambda z, x, h: ((z + 1) % plan.planes, x, h))
            terms.append((values[m], plan.partner(values[m], 0, 1)))
        steps.append((pieces, terms))
    total = None
    for index in range(0, len(steps) - 1, 2):
        part = steps[index : min(index + 2, len(steps) - 1)]
        total = weight_terms(plan, scal, total, part)
    near, far = [], []
    for m in range(2):
        (part,) = weight_terms(plan, scal, total, steps[-1:], m, 0)
        near.append(plan.send(part, lambda z, x, h: (z, h & 1, (h & ~1) | x)))
        (part,) = weight_terms(plan, scal, total, steps[-1:], m, 1)
        far.append(plan.send(part, lambda z, x, h: (z, h & 1, (h & ~1) | (x ^ 1))))
    return finish_weights(plan, scal, near, far)


def weight_gradient_summed(plan, scal, rows, own):
    h, x = scal[2], scal[1]
    half, dim, span = plan.half, plan.dim, plan.span
    mine = jnp.concatenate([own[0][:1], own[1][: half - 1]])
    other = jnp.concatenate([own[0][2:], own[1][half - 1 :]])
    other = plan.partner(other, 1, 0)
    low = jnp.where(x == 0, mine, other)
    high = jnp.where(x == 0, other, mine)
    value = jnp.concatenate([low, own[0][1:2], high], axis=0)
    value = value.reshape(plan.group * dim, plan.n_head, plan.block)
    places = jnp.arange(plan.n_head, dtype=jnp.int32) ^ (h & ~1)
    value = jnp.take(value, places, axis=1).reshape(plan.group * dim, span)
    gathered = lax.all_gather(rows, "head", axis=0, tiled=True)
    product = jnp.einsum("ts,ct->sc", gathered, value, preferred_element_type=F32)
    return lax.psum_scatter(product, "blk", scatter_dimension=0, tiled=True)


def local(n_blk, n_head, layer_input, queries, keys, values, out_grad, attn_out, log_sum, blocks):
    tokens, heads, dim = queries.shape
    plan = Plan(n_blk, n_head, heads // n_head, tokens, dim)
    n = n_head
    b, h = lax.axis_index("blk"), lax.axis_index("head")
    z, x, c = b // 2, b % 2, h % 2
    scal = jnp.stack([z, x, h, c]).astype(jnp.int32)
    z, x, h, c = scal[0], scal[1], scal[2], scal[3]
    by_head = lambda v: jnp.moveaxis(v, 1, 0)
    q, g, a, k, v = (by_head(m) for m in (queries, out_grad, attn_out, keys, values))

    mask = link_mask(plan, scal, blocks)
    sent = pack_queries(plan, scal, q, g, a, log_sum.T)
    windows = {(0, 0): sent[0]}
    for i, kk in [(1, kk) for kk in range(n)] + [(0, kk) for kk in range(1, n)]:
        windows[i, kk] = plan.partner(sent[i * n + kk], i, kk)
    pair_rows = STAT_ROWS + plan.half * 2 * tokens
    outward = lambda z, x, h: (z + 1 - 2 * x, x, h)
    inward = lambda z, x, h: (z - 1 + 2 * x, x, h)
    pairs = [(kk, kk + 1) for kk in range(0, n, 2)]


    def join(i, rows, kks):
        return jnp.concatenate([windows[i, kk][:rows] for kk in kks])

    all_rows = sent[0].shape[0]
    near = [plan.send(join(1, all_rows, kk), outward) for kk in pairs]
    far = [plan.send(join(0, pair_rows, kk), inward) for kk in pairs]
    packed = pack_keys(plan, scal, k, v)
    moved = [packed[0]]
    moved += [plan.partner(packed[kk], 0, kk) for kk in range(1, n)]
    moved += [plan.partner(packed[n + kk], 1, kk) for kk in range(n)]
    ordered = near + [windows[0, kk] for kk in range(n)] + [windows[1, kk] for kk in range(n)] + far

    own = [value_terms(plan, scal, mask, ordered, moved, m) for m in range(2)]
    inner = [windows[i, kk] for i in range(2) for kk in range(n)]
    near_part, mine0, dk0 = score_terms(plan, scal, mask, near + inner, moved[:n], 0)
    far_part, mine1, dk1 = score_terms(plan, scal, mask, inner + far, moved[n:], 1)
    near_sum = plan.send(near_part, inward)
    far_sum = plan.send(far_part, outward)
    back0 = pack_returns(plan, scal, 0, far_sum, (mine0, mine1), dk0)
    back1 = pack_returns(plan, scal, 1, near_sum, (mine0, mine1), dk1)
    back = [back0[0]]
    back += [plan.partner(back0[kk], 0, kk) for kk in range(1, n)]
    back += [plan.partner(back1[kk], 1, kk) for kk in range(n)]
    dq, dk = unpack_returns(plan, scal, back)
    few = plan.planes <= 4 and (layer_input.shape[1] // n_blk) % 128 == 0
    dw = (weight_gradient if few else weight_gradient_summed)(plan, scal, layer_input, own)
    return jnp.moveaxis(dq, 0, 1), jnp.moveaxis(dk, 0, 1), dw


def solution(mesh):
    rows = P(AXES, None)
    cube = P(AXES, None, None)
    body = functools.partial(local, mesh.shape["blk"], mesh.shape["head"])
    return jax.shard_map(
        body,
        mesh=mesh,
        in_specs=(rows, cube, cube, cube, cube, cube, rows, P()),
        out_specs=(cube, cube, P("blk", "head")),
        check_vma=False,
    )
```
